32 devices in a mesh: group: 2 (over x), ep: 16 (over z, y, core).
Axes of the slice: x: 2, y: 2, z: 4, core: 2. Of those that a mesh axis runs over, the one named last changes fastest.
Arguments:
- hidden: bfloat16 [4096, 2048], P(('group', 'ep')), parts along dimension 0, may hold values from -6 to 6
- norm_gain: float32 [2048], replicated, may hold values from 0.25 to 4
- routes: int32 [4096, 8], P(('group', 'ep')), parts along dimension 0, may hold values from 0 to 15, all different within a row; in each aligned block of 128 rows (0 to 127, 128 to 255, ...) at most 80 rows name the same one
- route_weight: float32 [4096, 8], P(('group', 'ep')), parts along dimension 0, may hold values from 0.05 to 1
- w_gate: bfloat16 [16, 2048, 768], P('ep'), may hold values from -0.125 to 0.125
- w_up: bfloat16 [16, 2048, 768], P('ep'), may hold values from -0.125 to 0.125
- w_down: bfloat16 [16, 768, 2048], P('ep'), may hold values from -0.21875 to 0.21875
Outputs:
- mixed: bfloat16 [4096, 2048], P(('group', 'ep')), parts along dimension 0
The draws below stay inside these ranges and needn't reach their ends.
There are 2 independent parts, one for each index of `group`. The reference program is written for one: setup_inputs(seed, part) draws one part's arguments, and reference() takes and returns one part's arrays. A program takes and returns all parts, laid end to end along the dimension named above; an argument that names none is the same for every part. Nothing has to cross between parts.
Inputs may be any that keep to these rules, and one draw needn't show every extreme that they name: `routes`: each row names 8 different experts. Among the rows of one device no expert is named more than 80 times, a bound that some block reaches.
All inputs are finite; a program needn't handle non-finite values.
Results may differ from the reference program's by a relative error of at most 0.0085.
Values may be sent and summed in bfloat16 or wider, within the bound.
A program may use at most 128 MiB of HBM per device.

```python
import math
import jax
import jax.numpy as jnp
import numpy as np
from jax import lax

D = 2048
FF = 768
TOP = 8
TOK_DEV = 128
EXPERTS = 16
TOKENS = 2048
CAP = 80
N_EP = 16


def block_levels(stream_key, shape, pieces, low, top_value):
    def one(dim, parts):
        draws = jax.random.uniform(jax.random.fold_in(jax.random.fold_in(stream_key, 6), dim), (parts,), jnp.float32, low / len(pieces), top_value / len(pieces))
        return jnp.repeat(jnp.exp(draws), shape[dim] // parts).reshape((-1,) + (1,) * (len(shape) - dim - 1))

    factor_of = one(*pieces[0])
    for cut in pieces[1:]:
        factor_of = factor_of * one(*cut)
    return factor_of


def shared_out(key, own, number, rows, amount, top, limit, lean):
    ranking = jax.random.permutation(key, amount)
    crowded, usual = load_shares(amount, rows * top, limit, lean, True), load_shares(amount, rows * top, limit, lean, False)
    places = jnp.arange(amount)

    def named(sizes, turn):
        used = int((sizes > 0).sum())
        fixed = max(1, used // 4)
        shifted = fixed + (places - fixed + turn * (used - fixed)) % max(1, amount - fixed)
        return jnp.zeros((amount,), jnp.int32).at[ranking[jnp.where(places < fixed, places, shifted)]].set(jnp.asarray(sizes, jnp.int32))

    sizes = jnp.where(number % 4 == 0, named(crowded, number // 4), named(usual, number - number // 4 - 1))
    mixed = jax.random.permutation(jax.random.fold_in(own, 3), amount)
    giver, taker = mixed[0:amount // 2 * 2:2], mixed[1:amount // 2 * 2:2]
    room = jnp.minimum(sizes[giver] - 1, limit - sizes[taker]) // 2
    room = jnp.where((giver == ranking[0]) | (taker == ranking[0]) | (sizes[taker] == 0), 0, jnp.maximum(room, 0))
    shifted = jax.random.randint(jax.random.fold_in(own, 4), (amount // 2,), 0, 1 << 20) % (room + 1)
    sizes = sizes.at[giver].add(-shifted).at[taker].add(shifted)
    labels = jnp.searchsorted(jnp.cumsum(sizes), jnp.arange(rows * top), side="right").astype(jnp.int32)
    grid = labels.reshape(top, rows).T
    grid = grid[jax.random.permutation(jax.random.fold_in(own, 1), rows)]
    turn = jax.random.randint(jax.random.fold_in(own, 2), (rows, 1), 0, top)
    return jnp.take_along_axis(grid, (jnp.arange(top)[None, :] + turn) % top, axis=1)


def load_shares(number_of, total, most, slope, full):
    loads = [(1 << 20) // math.isqrt(standing ** slope) + 1 for standing in range(1, number_of + 1)]
    largest = most if full else min(most, max(-(-total // number_of), total * loads[0] // sum(loads)))
    least = 1 if total - largest >= number_of - 1 else 0
    given, rest = [largest] + [least] * (number_of - 1), total - largest - least * (number_of - 1)
    while rest > 0:
        candidates = [i for i in range(1, number_of) if given[i] < largest] or [i for i in range(1, number_of) if given[i] < most]
        mass, remaining = sum([loads[i] for i in candidates]), rest
        for i in candidates:
            addition = min(most - given[i], max(1, remaining * loads[i] // mass), rest)
            given[i] = given[i] + addition
            rest = rest - addition
    return np.array(given)


def gaussian(rng, extent, width, limit, pieces=(), kind=jnp.bfloat16):
    values = width * jax.random.normal(rng, extent, jnp.float32)
    if pieces:
        values = values * block_levels(rng, extent, pieces, -0.22, 0.18)
    return jnp.clip(values, -limit, limit).astype(kind)


def setup_inputs(seed: int = 0, part: int = 0) -> dict:
    arg_keys = jax.random.split(jax.random.key(seed), 8)
    part_keys = jax.random.split(jax.random.fold_in(arg_keys[7], part), 8)
    hidden = gaussian(part_keys[0], (TOKENS, D), 1.0, 6.0, ((0, 16),))
    norm_gain = jnp.clip(jnp.exp(jax.random.uniform(arg_keys[1], (D,), jnp.float32, math.log(0.25), math.log(4.0))), 0.25, 4.0)
    routes_keys = jax.random.split(jax.random.fold_in(part_keys[2], 1), TOKENS // TOK_DEV)
    routes_turns = jax.random.permutation(jax.random.fold_in(part_keys[2], 3), TOKENS // TOK_DEV)
    routes = jax.vmap(lambda own, number: shared_out(jax.random.fold_in(part_keys[2], 2), own, number, TOK_DEV, EXPERTS, TOP, CAP, 2))(routes_keys, routes_turns).reshape((TOKENS, TOP))
    route_weight = jnp.clip(0.05 + 0.95 * jax.random.uniform(part_keys[3], (TOKENS, TOP), jnp.float32) ** block_levels(part_keys[3], (TOKENS, TOP), ((0, 16),), -0.2, 0.2), 0.05, 1.0)
    w_gate = gaussian(arg_keys[4], (EXPERTS, D, FF), D ** -0.5, 0.125, ((0, 16),))
    w_up = gaussian(arg_keys[5], (EXPERTS, D, FF), D ** -0.5, 0.125, ((0, 16),))
    w_down = gaussian(arg_keys[6], (EXPERTS, FF, D), FF ** -0.5, 0.21875, ((0, 16),))
    return dict(hidden=hidden, norm_gain=norm_gain, routes=routes, route_weight=route_weight, w_gate=w_gate, w_up=w_up, w_down=w_down)


def reference(hidden, norm_gain, routes, route_weight, w_gate, w_up, w_down):
    tokens_all = hidden.shape[0]
    n_src = N_EP
    tok = tokens_all // n_src
    xf = hidden.astype(jnp.float32)
    normed = (xf * lax.rsqrt(lax.optimization_barrier(jnp.mean(xf * xf, axis=-1, keepdims=True)) + 1e-06) * norm_gain).astype(jnp.bfloat16)
    share = route_weight / lax.optimization_barrier(jnp.sum(route_weight, axis=1, keepdims=True))
    flat = routes.reshape(n_src, tok * TOP)
    onehot = (flat[:, :, None] == jnp.arange(EXPERTS, dtype=jnp.int32)[None, None, :]).astype(jnp.int32)
    ranked = jnp.cumsum(onehot, axis=1) - onehot
    slot = lax.optimization_barrier(jnp.sum(ranked * onehot, axis=2)).astype(jnp.int32)
    source = jnp.broadcast_to(jnp.arange(n_src, dtype=jnp.int32)[:, None], (n_src, tok * TOP))
    token = source * tok + (jnp.arange(tok * TOP, dtype=jnp.int32) // TOP)[None, :]
    table = jnp.full((EXPERTS, n_src, CAP), tokens_all, jnp.int32).at[flat, source, slot].set(token.astype(jnp.int32))
    wtable = jnp.zeros((EXPERTS, n_src, CAP), jnp.float32).at[flat, source, slot].set(share.reshape(n_src, tok * TOP))
    padded = jnp.concatenate([normed, jnp.zeros((1, D), jnp.bfloat16)], axis=0)

    def expert_step(total, expert):
        index = table[expert].reshape(-1)
        rows = padded[index]
        gate = jnp.dot(rows, w_gate[expert], preferred_element_type=jnp.float32)
        upper = jnp.dot(rows, w_up[expert], preferred_element_type=jnp.float32)
        units = (jax.nn.silu(gate) * upper).astype(jnp.bfloat16)
        result = jnp.dot(units, w_down[expert], preferred_element_type=jnp.float32).astype(jnp.bfloat16)
        weighted = wtable[expert].reshape(-1)[:, None] * result.astype(jnp.float32)
        total = total.at[index].add(weighted, mode='drop')
        return (total, None)
    total, _ = lax.scan(expert_step, jnp.zeros((tokens_all, D), jnp.float32), jnp.arange(EXPERTS, dtype=jnp.int32))
    return total.astype(jnp.bfloat16)
```

```python
import functools

import jax
import jax.numpy as jnp
from jax import lax
from jax.experimental import pallas as pl
from jax.experimental.pallas import tpu as pltpu
from jax.sharding import PartitionSpec as P

MESH = pl.DeviceIdType.MESH
LANES = 128
F_TILE = 768
D_TILE = 512
VMEM_BYTES = 60 * 1024 * 1024


def exchange(hidden, norm_gain, routes, route_weight, w_gate, w_up, w_down):
    count = lax.axis_size("ep")
    tok = hidden.shape[0]
    width = hidden.shape[1]
    picks = routes.shape[1]
    experts = count * w_gate.shape[0]
    slots = tok * picks * 5 // (4 * experts)
    xf = hidden.astype(jnp.float32)
    normed = (xf * lax.rsqrt(jnp.mean(xf * xf, axis=-1, keepdims=True) + 1e-06) * norm_gain).astype(
        jnp.bfloat16
    )
    share = route_weight / jnp.sum(route_weight, axis=1, keepdims=True)
    flat = routes.reshape(-1)
    onehot = (flat[:, None] == jnp.arange(experts, dtype=jnp.int32)[None, :]).astype(jnp.int32)
    ranked = jnp.cumsum(onehot, axis=0) - onehot
    slot = jnp.sum(ranked * onehot, axis=1)
    token_of = jnp.arange(tok * picks, dtype=jnp.int32) // picks
    outgoing = jnp.zeros((experts, slots, width), jnp.bfloat16).at[flat, slot].set(normed[token_of])
    arrived = lax.all_to_all(outgoing, "ep", split_axis=0, concat_axis=0, tiled=True)
    rows = arrived.reshape(-1, width)
    gate = jnp.dot(rows, w_gate[0], preferred_element_type=jnp.float32)
    upper = jnp.dot(rows, w_up[0], preferred_element_type=jnp.float32)
    units = (jax.nn.silu(gate) * upper).astype(jnp.bfloat16)
    result = jnp.dot(units, w_down[0], preferred_element_type=jnp.float32).astype(jnp.bfloat16)
    coming_back = lax.all_to_all(
        result.reshape(arrived.shape), "ep", split_axis=0, concat_axis=0, tiled=True
    )
    picked = coming_back[flat, slot]
    picked = picked.reshape(tok, picks, width).astype(jnp.float32)
    mixed = jnp.einsum("tk,tkd->td", share, picked)
    return mixed.astype(jnp.bfloat16)


def ring_kernel(
    count,
    hidden_ref, gain_ref, routes_ref, score_ref, gate_hbm, up_hbm, down_hbm,
    out_ref,
    x, y, sib, rin, units, wcol, win, gate, up, down,
    ag_send, ag_recv, xs_send, xs_recv, wa_send, wa_recv, wx_send, wx_recv,
    ys_send, ys_recv, rs_send, rs_recv, load_sem,
):
    ring = count // 2
    last = ring // 2
    far = last - 1
    tok, width = hidden_ref.shape
    picks = routes_ref.shape[0]
    hidden_units = gate_hbm.shape[2]
    half = tok // 2
    quarter = half // 2
    f32, bf16 = jnp.float32, jnp.bfloat16

    me = lax.axis_index("ep")
    core = me % 2
    chip = me // 2
    side = chip % 2
    along = chip // 2
    pos = along + side * (ring - 1 - 2 * along)

    def device(position, c):
        p = (position + ring) % ring
        s = p // last
        a = p + s * (ring - 1 - 2 * p)
        return (a * 2 + s) * 2 + c

    towards = (device(pos + 1, core), device(pos - 1, core))
    sibling = device(pos, 1 - core)

    def shard(d, s):
        return 0 if s == 0 else ring - 1 if s == last else 2 * s - 1 + d

    def piece(d, s, h):
        if s in (0, last):
            return shard(d, s), h
        return 2 * s - 1 + (h != d), d

    def own_row(d, s, h):
        i, place = piece(d, s, h)
        return (4 * i + place) * half

    def sib_row(d, s, h):
        return own_row(d, s, h) + tok

    def rcopy(src, dst, ssem, rsem, target):
        return pltpu.make_async_remote_copy(
            src_ref=src, dst_ref=dst, send_sem=ssem, recv_sem=rsem,
            device_id={"ep": target}, device_id_type=MESH,
        )

    def ag(d, s, h):
        src = x.at[pl.ds(own_row(d, s - 1, h), half)]
        dst = x.at[pl.ds(own_row(d, s, h), half)]
        return rcopy(src, dst, ag_send.at[d, s - 1, h, 0], ag_recv.at[d, s - 1, h, 0], towards[d])

    def agq(d, s, q):
        src = x.at[pl.ds(own_row(d, s - 1, d) + q * quarter, quarter)]
        dst = x.at[pl.ds(own_row(d, s, d) + q * quarter, quarter)]
        return rcopy(src, dst, ag_send.at[d, s - 1, d, q], ag_recv.at[d, s - 1, d, q], towards[d])

    def xs(d, s, h):
        j = shard(d, s)
        src = x.at[pl.ds(own_row(d, s, h), half)]
        dst = x.at[pl.ds(sib_row(d, s, h), half)]
        return rcopy(src, dst, xs_send.at[j, h], xs_recv.at[j, h], sibling)

    def wa(d, s):
        j = shard(d, s)
        return rcopy(win.at[shard(d, s - 1)], win.at[j], wa_send.at[j], wa_recv.at[j], towards[d])

    def wx(d, s):
        j = shard(d, s)
        return rcopy(win.at[j], win.at[ring + j], wx_send.at[j], wx_recv.at[j], sibling)

    parts = 2
    span = width // parts

    def ys(i, part):
        cols = pl.ds(part * span, span)
        src = y.at[pl.ds((4 * i + 2) * half, tok), cols]
        dst = sib.at[pl.ds(i * tok, tok), cols]
        return rcopy(src, dst, ys_send.at[i, part], ys_recv.at[i, part], sibling)

    def rin_row(d, s, h):
        return ((d * last + s) * 2 + h) * half

    def rs(d, s, h, q):
        src = y.at[pl.ds(own_row(d, s, h) + q * quarter, quarter)]
        dst = rin.at[pl.ds(rin_row(d, s - 1, h) + q * quarter, quarter)]
        return rcopy(src, dst, rs_send.at[d, s - 1, h, q], rs_recv.at[d, s - 1, h, q], towards[1 - d])

    barrier = pltpu.get_barrier_semaphore()
    for target in (*towards, sibling):
        pl.semaphore_signal(barrier, inc=1, device_id={"ep": target}, device_id_type=MESH)

    loads = [
        pltpu.make_async_copy(src.at[0], dst, load_sem.at[i])
        for i, (src, dst) in enumerate(((gate_hbm, gate), (up_hbm, up), (down_hbm, down)))
    ]

    gain = gain_ref[...]
    for h in range(2):
        xf = hidden_ref[pl.ds(half * h, half), :].astype(f32)
        scale = lax.rsqrt(jnp.mean(xf * xf, axis=-1, keepdims=True) + 1e-06)
        x[pl.ds(half * h, half), :] = (xf * scale * gain).astype(bf16)
        if h == 0:
            pl.semaphore_wait(barrier, 3)
        ag(1 - h, 1, h).start()
        xs(0, 0, h).start()

    for d in range(2):
        ag(d, 1, d).start()
    for load in loads:
        load.start()
    score = score_ref[...]
    share = score / jnp.sum(score, axis=0, keepdims=True)
    expert = lax.broadcasted_iota(jnp.int32, (count, tok), 0)
    dense = jnp.zeros((count, tok), f32)
    for k in range(picks):
        dense += jnp.where(routes_ref[k : k + 1, :] == expert, share[k : k + 1, :], 0.0)
    for e in range(count):
        win[0, e] = dense[e : e + 1, :]
    for d in range(2):
        wa(d, 1).start()
    wx(0, 0).start()

    f_tile = F_TILE if hidden_units % F_TILE == 0 else LANES
    d_tile = D_TILE if span % D_TILE == 0 else LANES
    rows = 2 * tok

    def spread(d, s):
        j = shard(d, s)
        for slot, row_of in ((j, own_row), (ring + j, sib_row)):
            w = jnp.transpose(jnp.broadcast_to(win[slot, me], (LANES, tok)))
            for h in range(2):
                row = row_of(d, s, h)
                wcol[row : row + half, :] = w[half * h : half * (h + 1), :]

    def hidden_part(i):
        row0 = i * rows

        def first(n, carry):
            cols = pl.ds(pl.multiple_of(n * f_tile, f_tile), f_tile)
            g = jnp.dot(x[row0 : row0 + rows, :], gate[:, cols], preferred_element_type=f32)
            u = jnp.dot(x[row0 : row0 + rows, :], up[:, cols], preferred_element_type=f32)
            units[:, cols] = (g / (1.0 + jnp.exp(-g)) * u).astype(bf16)
            return carry

        lax.fori_loop(0, hidden_units // f_tile, first, 0)

    def result_part(i):
        row0 = i * rows

        def second(n, carry):
            cols = pl.ds(pl.multiple_of(n * d_tile, d_tile), d_tile)
            r = jnp.dot(units[...], down[:, cols], preferred_element_type=f32)
            w = wcol[row0 : row0 + rows, :]
            for q in range(d_tile // LANES):
                part = pl.ds(pl.multiple_of(n * d_tile + q * LANES, LANES), LANES)
                y[row0 : row0 + rows, part] = (r[:, q * LANES : (q + 1) * LANES] * w).astype(bf16)
            return carry

        steps = span // d_tile
        for part in range(parts):
            lax.fori_loop(part * steps, (part + 1) * steps, second, 0)
            ys(i, part).start()

    def compute(i):
        hidden_part(i)
        result_part(i)

    seen = set()

    def await_results(i):
        if i not in seen:
            seen.add(i)
            for part in range(parts):
                ys(i, part).wait_recv()

    def combine(s, lead, quarters=(0, 1)):
        for q in quarters:
            for d in range(2):
                h = d if lead else 1 - d
                i, _ = piece(d, s, h)
                await_results(i)
                row = own_row(d, s, h) + q * quarter
                other = row - (2 * i) * half
                total = y[row : row + quarter, :].astype(f32)
                total += sib[other : other + quarter, :].astype(f32)
                if s < far or (s == far and lead):
                    rs(d, s + 1, h, q).wait_recv()
                    total += rin[pl.ds(rin_row(d, s, h) + q * quarter, quarter), :].astype(f32)
                y[row : row + quarter, :] = total.astype(bf16)
                rs(d, s, h, q).start()

    def ready(s, lead):
        for d in range(2):
            xs(d, s, d if lead else 1 - d).wait_recv()

    late = 1

    wx(0, 0).wait_recv()
    spread(0, 0)
    for load in loads:
        load.wait()
    for h in range(2):
        xs(0, 0, h).wait_recv()
    compute(0)

    for s in range(1, last):
        for d in range(2):
            ag(d, s, 1 - d).wait_recv()
            if s < far:
                ag(d, s + 1, 1 - d).start()
            xs(d, s, 1 - d).start()
            wa(d, s).wait_recv()
            if s < far or d == 0:
                wa(d, s + 1).start()
            wx(d, s).start()
        for d in range(2):
            wx(d, s).wait_recv()
            spread(d, s)
        ready(s, False)
        hidden_part(2 * s)
        if s == far:
            for d in range(2):
                agq(d, s, 0).wait_recv()
                agq(d, s + 1, 0).start()
        result_part(2 * s)
        for d in range(2):
            if s == far:
                agq(d, s, 1).wait_recv()
                agq(d, s + 1, 1).start()
            else:
                ag(d, s, d).wait_recv()
                if s + 1 == far:
                    for q in range(2):
                        agq(d, s + 1, q).start()
                else:
                    ag(d, s + 1, d).start()
            xs(d, s, d).start()
        if s == far:
            combine(far, False)
        if s != late:
            ready(s, True)
            compute(2 * s - 1)

    wa(0, last).wait_recv()
    wx(0, last).start()
    for d in range(2):
        for q in range(2):
            agq(d, last, q).wait_recv()
        xs(d, last, d).start()
    wx(0, last).wait_recv()
    spread(0, last)
    ready(last, True)
    hidden_part(ring - 1)
    combine(far - 1, False, (0,))
    result_part(ring - 1)
    combine(far - 1, False, (1,))
    combine(last, True)
    ready(late, True)
    compute(2 * late - 1)
    combine(far, True)
    for s in range(far - 1, 0, -1):
        if s > 1:
            combine(s - 1, False)
        combine(s, True)
    await_results(0)
    for q in range(2):
        for h in range(2):
            row = h * half + q * quarter
            total = y[row : row + quarter, :].astype(f32)
            total += sib[row : row + quarter, :].astype(f32)
            for d in (1 - h, h):
                rs(d, 1, h, q).wait_recv()
                total += rin[pl.ds(rin_row(d, 0, h) + q * quarter, quarter), :].astype(f32)
            out_ref[row : row + quarter, :] = total.astype(out_ref.dtype)

    for d in range(2):
        for s in range(1, last + 1):
            if s < last or d == 0:
                wa(d, s).wait_send()
            for h in range(2):
                if s < last or h == d:
                    if s >= far and h == d:
                        for q in range(2):
                            agq(d, s, q).wait_send()
                    else:
                        ag(d, s, h).wait_send()
                    for q in range(2):
                        rs(d, s, h, q).wait_send()
    for s in range(last + 1):
        for d in range(1 if s in (0, last) else 2):
            wx(d, s).wait_send()
            for h in range(2):
                xs(d, s, h).wait_send()
    for i in range(ring):
        for part in range(parts):
            ys(i, part).wait_send()


def ring_body(count, hidden, norm_gain, routes, route_weight, w_gate, w_up, w_down):
    tok, width = hidden.shape
    ring = count // 2
    last = ring // 2
    hidden_units = w_gate.shape[2]
    vmem = pl.BlockSpec(memory_space=pltpu.VMEM)
    hbm = pl.BlockSpec(memory_space=pl.ANY)
    bf16, f32 = jnp.bfloat16, jnp.float32
    dma = pltpu.SemaphoreType.DMA
    return pl.pallas_call(
        functools.partial(ring_kernel, count),
        out_shape=jax.ShapeDtypeStruct((tok, width), bf16),
        in_specs=[vmem] * 4 + [hbm] * 3,
        out_specs=vmem,
        scratch_shapes=[
            pltpu.VMEM((count * tok, width), bf16),
            pltpu.VMEM((count * tok, width), bf16),
            pltpu.VMEM((ring * tok, width), bf16),
            pltpu.VMEM((2 * last * tok, width), bf16),
            pltpu.VMEM((2 * tok, hidden_units), bf16),
            pltpu.VMEM((count * tok, LANES), f32),
            pltpu.VMEM((count, count, 1, tok), f32),
            pltpu.VMEM(w_gate.shape[1:], bf16),
            pltpu.VMEM(w_up.shape[1:], bf16),
            pltpu.VMEM(w_down.shape[1:], bf16),
            dma((2, last, 2, 2)), dma((2, last, 2, 2)),
            dma((ring, 2)), dma((ring, 2)),
            dma((ring,)), dma((ring,)),
            dma((ring,)), dma((ring,)),
            dma((ring, 2)), dma((ring, 2)),
            dma((2, last, 2, 2)), dma((2, last, 2, 2)),
            dma((3,)),
        ],
        compiler_params=pltpu.CompilerParams(
            collective_id=0, has_side_effects=True, vmem_limit_bytes=VMEM_BYTES
        ),
    )(hidden, norm_gain.reshape(1, width), routes.T, route_weight.T, w_gate, w_up, w_down)


def fits(count, tok, width, units, picks):
    rows = count * tok
    held = 2 * (3 * rows * width + 3 * width * units) + 4 * tok * units + 8 * rows * LANES
    dense = count <= 2 * picks and count <= LANES
    return dense and count % 4 == 0 and count >= 16 and held < VMEM_BYTES * 3 // 4


def solution(mesh):
    count = mesh.shape["ep"]

    def body(*args):
        hidden, routes, w_gate = args[0], args[2], args[4]
        if fits(count, *hidden.shape, w_gate.shape[2], routes.shape[1]):
            return ring_body(count, *args)
        return exchange(*args)

    in_specs = (
        P(("group", "ep"), None),
        P(),
        P(("group", "ep"), None),
        P(("group", "ep"), None),
        P("ep", None, None),
        P("ep", None, None),
        P("ep", None, None),
    )
    out_specs = P(("group", "ep"), None)
    return jax.shard_map(body, mesh=mesh, in_specs=in_specs, out_specs=out_specs, check_vma=False)
```

```python
import functools

import jax
import jax.numpy as jnp
from jax import lax
from jax.experimental import pallas as pl
from jax.experimental.pallas import tpu as pltpu
from jax.sharding import PartitionSpec as P

MESH = pl.DeviceIdType.MESH
LANES = 128
F_TILE = 768
D_TILE = 512
VMEM_BYTES = 60 * 1024 * 1024


def exchange(hidden, norm_gain, routes, route_weight, w_gate, w_up, w_down):
    count = lax.axis_size("ep")
    tok = hidden.shape[0]
    width = hidden.shape[1]
    picks = routes.shape[1]
    experts = count * w_gate.shape[0]
    slots = tok * picks * 5 // (4 * experts)
    xf = hidden.astype(jnp.float32)
    normed = (xf * lax.rsqrt(jnp.mean(xf * xf, axis=-1, keepdims=True) + 1e-06) * norm_gain).astype(
        jnp.bfloat16
    )
    share = route_weight / jnp.sum(route_weight, axis=1, keepdims=True)
    flat = routes.reshape(-1)
    onehot = (flat[:, None] == jnp.arange(experts, dtype=jnp.int32)[None, :]).astype(jnp.int32)
    ranked = jnp.cumsum(onehot, axis=0) - onehot
    slot = jnp.sum(ranked * onehot, axis=1)
    token_of = jnp.arange(tok * picks, dtype=jnp.int32) // picks
    outgoing = jnp.zeros((experts, slots, width), jnp.bfloat16).at[flat, slot].set(normed[token_of])
    arrived = lax.all_to_all(outgoing, "ep", split_axis=0, concat_axis=0, tiled=True)
    rows = arrived.reshape(-1, width)
    gate = jnp.dot(rows, w_gate[0], preferred_element_type=jnp.float32)
    upper = jnp.dot(rows, w_up[0], preferred_element_type=jnp.float32)
    units = (jax.nn.silu(gate) * upper).astype(jnp.bfloat16)
    result = jnp.dot(units, w_down[0], preferred_element_type=jnp.float32).astype(jnp.bfloat16)
    coming_back = lax.all_to_all(
        result.reshape(arrived.shape), "ep", split_axis=0, concat_axis=0, tiled=True
    )
    picked = coming_back[flat, slot]
    picked = picked.reshape(tok, picks, width).astype(jnp.float32)
    mixed = jnp.einsum("tk,tkd->td", share, picked)
    return mixed.astype(jnp.bfloat16)


def ring_kernel(
    count,
    hidden_hbm, gain_ref, routes_ref, score_ref, gate_hbm, up_hbm, down_hbm,
    out_ref,
    raw, x, y, sib, rin, units, wcol, win, gate, up, down,
    ag_send, ag_recv, xs_send, xs_recv, wa_send, wa_recv, wx_send, wx_recv,
    ys_send, ys_recv, rs_send, rs_recv, load_sem, raw_sem,
):
    ring = count // 2
    last = ring // 2
    far = last - 1
    tok, width = hidden_hbm.shape
    picks = routes_ref.shape[0]
    hidden_units = gate_hbm.shape[2]
    half = tok // 2
    quarter = half // 2
    f32, bf16 = jnp.float32, jnp.bfloat16

    me = lax.axis_index("ep")
    core = me % 2
    chip = me // 2
    side = chip % 2
    along = chip // 2
    pos = along + side * (ring - 1 - 2 * along)

    def device(position, c):
        p = (position + ring) % ring
        s = p // last
        a = p + s * (ring - 1 - 2 * p)
        return (a * 2 + s) * 2 + c

    towards = (device(pos + 1, core), device(pos - 1, core))
    sibling = device(pos, 1 - core)

    def shard(d, s):
        return 0 if s == 0 else ring - 1 if s == last else 2 * s - 1 + d

    def piece(d, s, h):
        if s in (0, last):
            return shard(d, s), h
        return 2 * s - 1 + (h != d), d

    def own_row(d, s, h):
        i, place = piece(d, s, h)
        return (4 * i + place) * half

    def sib_row(d, s, h):
        return own_row(d, s, h) + tok

    def rcopy(src, dst, ssem, rsem, target):
        return pltpu.make_async_remote_copy(
            src_ref=src, dst_ref=dst, send_sem=ssem, recv_sem=rsem,
            device_id={"ep": target}, device_id_type=MESH,
        )

    def ag(d, s, h):
        src = x.at[pl.ds(own_row(d, s - 1, h), half)]
        dst = x.at[pl.ds(own_row(d, s, h), half)]
        return rcopy(src, dst, ag_send.at[d, s - 1, h, 0], ag_recv.at[d, s - 1, h, 0], towards[d])

    def agq(d, s, q):
        src = x.at[pl.ds(own_row(d, s - 1, d) + q * quarter, quarter)]
        dst = x.at[pl.ds(own_row(d, s, d) + q * quarter, quarter)]
        return rcopy(src, dst, ag_send.at[d, s - 1, d, q], ag_recv.at[d, s - 1, d, q], towards[d])

    def xs(d, s, h):
        j = shard(d, s)
        src = x.at[pl.ds(own_row(d, s, h), half)]
        dst = x.at[pl.ds(sib_row(d, s, h), half)]
        return rcopy(src, dst, xs_send.at[j, h], xs_recv.at[j, h], sibling)

    def wa(d, s):
        j = shard(d, s)
        return rcopy(win.at[shard(d, s - 1)], win.at[j], wa_send.at[j], wa_recv.at[j], towards[d])

    def wx(d, s):
        j = shard(d, s)
        return rcopy(win.at[j], win.at[ring + j], wx_send.at[j], wx_recv.at[j], sibling)

    parts = 2
    span = width // parts

    def ys(i, part):
        cols = pl.ds(part * span, span)
        src = y.at[pl.ds((4 * i + 2) * half, tok), cols]
        dst = sib.at[pl.ds(i * tok, tok), cols]
        return rcopy(src, dst, ys_send.at[i, part], ys_recv.at[i, part], sibling)

    def rin_row(d, s, h):
        return ((d * last + s) * 2 + h) * half

    def rs(d, s, h, q):
        src = y.at[pl.ds(own_row(d, s, h) + q * quarter, quarter)]
        dst = rin.at[pl.ds(rin_row(d, s - 1, h) + q * quarter, quarter)]
        return rcopy(src, dst, rs_send.at[d, s - 1, h, q], rs_recv.at[d, s - 1, h, q], towards[1 - d])

    tokens = [
        pltpu.make_async_copy(
            hidden_hbm.at[pl.ds(half * h, half)], raw.at[pl.ds(half * h, half)], raw_sem.at[h]
        )
        for h in range(2)
    ]
    for load in tokens:
        load.start()
    barrier = pltpu.get_barrier_semaphore()
    for target in (*towards, sibling):
        pl.semaphore_signal(barrier, inc=1, device_id={"ep": target}, device_id_type=MESH)

    loads = [
        pltpu.make_async_copy(src.at[0], dst, load_sem.at[i])
        for i, (src, dst) in enumerate(((gate_hbm, gate), (up_hbm, up), (down_hbm, down)))
    ]

    gain = gain_ref[...]
    for h in range(2):
        tokens[h].wait()
        xf = raw[pl.ds(half * h, half), :].astype(f32)
        scale = lax.rsqrt(jnp.mean(xf * xf, axis=-1, keepdims=True) + 1e-06)
        x[pl.ds(half * h, half), :] = (xf * scale * gain).astype(bf16)
        if h == 0:
            pl.semaphore_wait(barrier, 3)
        ag(1 - h, 1, h).start()
        xs(0, 0, h).start()

    for d in range(2):
        ag(d, 1, d).start()
    for load in loads:
        load.start()
    score = score_ref[...]
    share = score / jnp.sum(score, axis=0, keepdims=True)
    expert = lax.broadcasted_iota(jnp.int32, (count, tok), 0)
    dense = jnp.zeros((count, tok), f32)
    for k in range(picks):
        dense += jnp.where(routes_ref[k : k + 1, :] == expert, share[k : k + 1, :], 0.0)
    for e in range(count):
        win[0, e] = dense[e : e + 1, :]
    for d in range(2):
        wa(d, 1).start()
    wx(0, 0).start()

    f_tile = F_TILE if hidden_units % F_TILE == 0 else LANES
    d_tile = D_TILE if span % D_TILE == 0 else LANES
    rows = 2 * tok

    def spread(d, s):
        j = shard(d, s)
        for slot, row_of in ((j, own_row), (ring + j, sib_row)):
            w = jnp.transpose(jnp.broadcast_to(win[slot, me], (LANES, tok)))
            for h in range(2):
                row = row_of(d, s, h)
                wcol[row : row + half, :] = w[half * h : half * (h + 1), :]

    def hidden_part(i):
        row0 = i * rows

        def first(n, carry):
            cols = pl.ds(pl.multiple_of(n * f_tile, f_tile), f_tile)
            g = jnp.dot(x[row0 : row0 + rows, :], gate[:, cols], preferred_element_type=f32)
            u = jnp.dot(x[row0 : row0 + rows, :], up[:, cols], preferred_element_type=f32)
            units[:, cols] = (g / (1.0 + jnp.exp(-g)) * u).astype(bf16)
            return carry

        lax.fori_loop(0, hidden_units // f_tile, first, 0)

    def result_part(i):
        row0 = i * rows

        def second(n, carry):
            cols = pl.ds(pl.multiple_of(n * d_tile, d_tile), d_tile)
            r = jnp.dot(units[...], down[:, cols], preferred_element_type=f32)
            w = wcol[row0 : row0 + rows, :]
            for q in range(d_tile // LANES):
                part = pl.ds(pl.multiple_of(n * d_tile + q * LANES, LANES), LANES)
                y[row0 : row0 + rows, part] = (r[:, q * LANES : (q + 1) * LANES] * w).astype(bf16)
            return carry

        steps = span // d_tile
        for part in range(parts):
            lax.fori_loop(part * steps, (part + 1) * steps, second, 0)
            ys(i, part).start()

    def compute(i):
        hidden_part(i)
        result_part(i)

    seen = set()

    def await_results(i):
        if i not in seen:
            seen.add(i)
            for part in range(parts):
                ys(i, part).wait_recv()

    def combine(s, lead, quarters=(0, 1)):
        for q in quarters:
            for d in range(2):
                h = d if lead else 1 - d
                i, _ = piece(d, s, h)
                await_results(i)
                row = own_row(d, s, h) + q * quarter
                other = row - (2 * i) * half
                total = y[row : row + quarter, :].astype(f32)
                total += sib[other : other + quarter, :].astype(f32)
                if s < far or (s == far and lead):
                    rs(d, s + 1, h, q).wait_recv()
                    total += rin[pl.ds(rin_row(d, s, h) + q * quarter, quarter), :].astype(f32)
                y[row : row + quarter, :] = total.astype(bf16)
                rs(d, s, h, q).start()

    def ready(s, lead):
        for d in range(2):
            xs(d, s, d if lead else 1 - d).wait_recv()

    def settle(i):
        s, lead = (i + 1) // 2, i % 2 == 1
        for d in range(2):
            xs(d, s, d if lead or i == 0 else 1 - d).wait_recv()
        compute(i)

    wx(0, 0).wait_recv()
    spread(0, 0)
    for load in loads:
        load.wait()

    held = (0, 1, 2, 3)
    for s in range(1, last):
        for d in range(2):
            ag(d, s, 1 - d).wait_recv()
            if s < far:
                ag(d, s + 1, 1 - d).start()
            xs(d, s, 1 - d).start()
            wa(d, s).wait_recv()
            if s < far or d == 0:
                wa(d, s + 1).start()
            wx(d, s).start()
        for d in range(2):
            wx(d, s).wait_recv()
            spread(d, s)
        if s == far:
            ready(s, False)
            hidden_part(2 * s)
            for d in range(2):
                agq(d, s, 0).wait_recv()
                agq(d, s + 1, 0).start()
            result_part(2 * s)
        elif 2 * s not in held:
            settle(2 * s)
        for d in range(2):
            if s == far:
                agq(d, s, 1).wait_recv()
                agq(d, s + 1, 1).start()
            else:
                ag(d, s, d).wait_recv()
                if s + 1 == far:
                    for q in range(2):
                        agq(d, s + 1, q).start()
                else:
                    ag(d, s + 1, d).start()
            xs(d, s, d).start()
        if s == far:
            combine(far, False)
        if 2 * s - 1 not in held:
            settle(2 * s - 1)

    wa(0, last).wait_recv()
    wx(0, last).start()
    for d in range(2):
        for q in range(2):
            agq(d, last, q).wait_recv()
        xs(d, last, d).start()
    wx(0, last).wait_recv()
    spread(0, last)
    ready(last, True)
    hidden_part(ring - 1)
    combine(far - 1, False, (0,))
    result_part(ring - 1)
    combine(far - 1, False, (1,))
    combine(last, True)
    settle(2)
    combine(far, True)
    settle(3)
    combine(1, False)
    combine(2, True)
    settle(1)
    settle(0)
    combine(1, True)
    await_results(0)
    for q in range(2):
        for h in range(2):
            row = h * half + q * quarter
            total = y[row : row + quarter, :].astype(f32)
            total += sib[row : row + quarter, :].astype(f32)
            for d in (1 - h, h):
                rs(d, 1, h, q).wait_recv()
                total += rin[pl.ds(rin_row(d, 0, h) + q * quarter, quarter), :].astype(f32)
            out_ref[row : row + quarter, :] = total.astype(out_ref.dtype)

    for d in range(2):
        for s in range(1, last + 1):
            if s < last or d == 0:
                wa(d, s).wait_send()
            for h in range(2):
                if s < last or h == d:
                    if s >= far and h == d:
                        for q in range(2):
                            agq(d, s, q).wait_send()
                    else:
                        ag(d, s, h).wait_send()
                    for q in range(2):
                        rs(d, s, h, q).wait_send()
    for s in range(last + 1):
        for d in range(1 if s in (0, last) else 2):
            wx(d, s).wait_send()
            for h in range(2):
                xs(d, s, h).wait_send()
    for i in range(ring):
        for part in range(parts):
            ys(i, part).wait_send()


def ring_body(count, hidden, norm_gain, routes, route_weight, w_gate, w_up, w_down):
    tok, width = hidden.shape
    ring = count // 2
    last = ring // 2
    hidden_units = w_gate.shape[2]
    vmem = pl.BlockSpec(memory_space=pltpu.VMEM)
    hbm = pl.BlockSpec(memory_space=pl.ANY)
    bf16, f32 = jnp.bfloat16, jnp.float32
    dma = pltpu.SemaphoreType.DMA
    return pl.pallas_call(
        functools.partial(ring_kernel, count),
        out_shape=pltpu.VMEM((tok, width), bf16),
        in_specs=[hbm] + [vmem] * 3 + [hbm] * 3,
        out_specs=vmem,
        scratch_shapes=[
            pltpu.VMEM((tok, width), bf16),
            pltpu.VMEM((count * tok, width), bf16),
            pltpu.VMEM((count * tok, width), bf16),
            pltpu.VMEM((ring * tok, width), bf16),
            pltpu.VMEM((2 * last * tok, width), bf16),
            pltpu.VMEM((2 * tok, hidden_units), bf16),
            pltpu.VMEM((count * tok, LANES), f32),
            pltpu.VMEM((count, count, 1, tok), f32),
            pltpu.VMEM(w_gate.shape[1:], bf16),
            pltpu.VMEM(w_up.shape[1:], bf16),
            pltpu.VMEM(w_down.shape[1:], bf16),
            dma((2, last, 2, 2)), dma((2, last, 2, 2)),
            dma((ring, 2)), dma((ring, 2)),
            dma((ring,)), dma((ring,)),
            dma((ring,)), dma((ring,)),
            dma((ring, 2)), dma((ring, 2)),
            dma((2, last, 2, 2)), dma((2, last, 2, 2)),
            dma((3,)), dma((2,)),
        ],
        compiler_params=pltpu.CompilerParams(
            collective_id=0, has_side_effects=True, vmem_limit_bytes=VMEM_BYTES
        ),
    )(hidden, norm_gain.reshape(1, width), routes.T, route_weight.T, w_gate, w_up, w_down)


def fits(count, tok, width, units, picks):
    rows = count * tok
    held = 2 * (3 * rows * width + 3 * width * units) + 4 * tok * units + 8 * rows * LANES
    dense = count <= 2 * picks and count <= LANES
    return dense and count % 4 == 0 and count >= 16 and held < VMEM_BYTES * 3 // 4


def solution(mesh):
    count = mesh.shape["ep"]

    def body(*args):
        hidden, routes, w_gate = args[0], args[2], args[4]
        if fits(count, *hidden.shape, w_gate.shape[2], routes.shape[1]):
            return ring_body(count, *args)
        return exchange(*args)

    in_specs = (
        P(("group", "ep"), None),
        P(),
        P(("group", "ep"), None),
        P(("group", "ep"), None),
        P("ep", None, None),
        P("ep", None, None),
        P("ep", None, None),
    )
    out_specs = P(("group", "ep"), None)
    return jax.shard_map(body, mesh=mesh, in_specs=in_specs, out_specs=out_specs, check_vma=False)
```
